32 devices in a mesh: cyc: 4 (over z), tile: 8 (over y, x, core).
Axes of the slice: x: 2, y: 2, z: 4, core: 2. Of those that a mesh axis runs over, the one named last changes fastest.
Arguments:
- weight_change: bfloat16 [4, 80, 80, 256], P('cyc', None, None, 'tile'), may hold values from -0.1796875 to 0.1796875
- ensemble: bfloat16 [4, 80, 8, 4096], P('cyc', None, None, 'tile'), may hold values from -6 to 6
- stencil_index: int32 [4, 4096], P(None, 'tile'), may hold values from 0 to 39
- stencil_weight: float32 [4, 4096], P(None, 'tile'), may hold values from 0.1 to 1
Outputs:
- smoothed: bfloat16 [4, 80, 8, 4096], P('cyc', None, None, 'tile')
The draws below stay inside these ranges and needn't reach their ends.
Inputs may be any that keep to these rules, and one draw needn't show every extreme that they name: `stencil_index`: positions 0 to 3 of the extended list are the last columns of the sector before (periodic in longitude), positions 36 and beyond the first columns of the sector after.
All inputs are finite; a program needn't handle non-finite values.
Results may differ from the reference program's by a relative error of at most 0.0085.
Values may be sent and summed in bfloat16 or wider, within the bound.
A program may use at most 128 MiB of HBM per device.

```python
import jax
import jax.numpy as jnp
from jax import lax

MEMBERS = 80
RIM_COLS = 4
COLS_DEV = 32
FINE_DEV = 512
CYCLES = 4
COLUMNS = 256
POINTS = 4096
CHANNELS = 8
N_TILE = 8


def with_ends(array, rng, smallest, top_value):
    longest = array.shape.index(max(array.shape))
    spots = []
    for shift in (0, 1):
        where = [jax.random.randint(jax.random.fold_in(rng, axis), (), 0, length) for axis, length in enumerate(array.shape)]
        where[longest] = (where[longest] + shift) % array.shape[longest]
        spots.append(tuple(where))
    return array.at[spots[0]].set(smallest).at[spots[1]].set(top_value)


def steps_of(key, shape, pieces, least, largest):
    gain = 1.0
    for axis_at, blocks in pieces:
        heights = jax.random.uniform(jax.random.fold_in(jax.random.fold_in(key, 6), axis_at), (blocks,), jnp.float32, least / len(pieces), largest / len(pieces))
        gain = gain * jnp.repeat(jnp.exp(heights), shape[axis_at] // blocks).reshape((-1,) + (1,) * (len(shape) - 1 - axis_at))
    return gain


def bell_draw(rng, dims, scale, most, cuts=(), held_as=jnp.bfloat16):
    array = scale * jax.random.normal(rng, dims, jnp.float32)
    if cuts:
        array = array * steps_of(rng, dims, cuts, -0.22, 0.18)
    return jnp.clip(array, -most, most).astype(held_as)


def setup_inputs(seed: int = 0) -> dict:
    streams_of = jax.random.split(jax.random.key(seed), 5)
    return {
        "weight_change": bell_draw(streams_of[0], (CYCLES, MEMBERS, MEMBERS, COLUMNS), 0.03, 0.1796875, ((0, 4), (3, 8))),
        "ensemble": bell_draw(streams_of[1], (CYCLES, MEMBERS, CHANNELS, POINTS), 1.0, 6.0, ((0, 4), (3, 8))),
        "stencil_index": with_ends(jax.random.randint(streams_of[2], (4, POINTS), 0, COLS_DEV + 2 * RIM_COLS), jax.random.fold_in(streams_of[2], 1), 0, (COLS_DEV + 2 * RIM_COLS) - 1).astype(jnp.int32),
        "stencil_weight": jnp.clip(0.1 + 0.9 * jax.random.uniform(streams_of[3], (4, POINTS), jnp.float32) ** steps_of(streams_of[3], (4, POINTS), ((1, 8),), -0.2, 0.2), 0.1, 1.0),
    }


def chain_sector(mats):
    members = mats.shape[1]
    eye = jnp.eye(members, dtype=jnp.float32)[:, :, None]
    start = jnp.broadcast_to(eye, mats.shape[1:])

    def later(carry, weight):
        product = jnp.einsum('ijg,jkg->ikg', weight, carry, precision=lax.Precision.HIGHEST, preferred_element_type=jnp.float32)
        return product, carry

    final, suffix = lax.scan(later, start, mats, reverse=True)
    return suffix


def apply_cycle(inputs, index, shares):
    products, states = inputs
    picked = jnp.take(products, index, axis=2)
    interp = jnp.sum(picked * shares[None, None, :, :], axis=2).astype(jnp.bfloat16)
    mixed = jnp.einsum('nvf,nmf->mvf', states.astype(jnp.float32), interp.astype(jnp.float32), precision=lax.Precision.HIGHEST)
    return mixed.astype(jnp.bfloat16)


def reference(weight_change, ensemble, stencil_index, stencil_weight):
    members = weight_change.shape[1]
    eye = jnp.eye(members, dtype=jnp.float32)[None, :, :, None]
    width = COLS_DEV + 2 * RIM_COLS
    offsets = jnp.arange(width).astype(jnp.int32)

    def sector(tile):
        columns = (tile * COLS_DEV - RIM_COLS + offsets + COLUMNS) % COLUMNS
        raw = jnp.take(weight_change, columns.astype(jnp.int32), axis=3)
        mats = raw.astype(jnp.float32) + eye
        suffix = chain_sector(mats)
        begin = (tile * FINE_DEV).astype(jnp.int32)
        index = lax.dynamic_slice_in_dim(stencil_index, begin, FINE_DEV, 1)
        weights = lax.dynamic_slice_in_dim(stencil_weight, begin, FINE_DEV, 1)
        shares = weights / jnp.sum(weights, axis=0, keepdims=True)
        states = lax.dynamic_slice_in_dim(ensemble, begin, FINE_DEV, 3)
        return lax.map(lambda pair: apply_cycle(pair, index, shares), (suffix, states))

    tiles = jnp.arange(N_TILE).astype(jnp.int32)
    result = lax.map(sector, tiles)
    result = jnp.moveaxis(result, 0, 3)
    return result.reshape(CYCLES, members, CHANNELS, N_TILE * FINE_DEV)
```

```python
import functools

import jax
import jax.numpy as jnp
from jax import lax
from jax.experimental import pallas as pl
from jax.experimental.pallas import tpu as pltpu
from jax.sharding import PartitionSpec as P

RIM_COLS = 4
CHUNK = 8
MESH = pl.DeviceIdType.MESH


def round_up(value, step):
    return -(-value // step) * step


def plan_of(members, columns):
    half = round_up(RIM_COLS * members, 128)
    edge = [(i * members, i) for i in range(RIM_COLS)]
    edge += [(half + i * members, columns - RIM_COLS + i) for i in range(RIM_COLS)]
    chunks = [(0, 2 * half, edge)]
    start = 2 * half
    for first in range(RIM_COLS, columns - RIM_COLS, CHUNK):
        count = min(CHUNK, columns - RIM_COLS - first)
        width = round_up(count * members, 128)
        chunks.append((start, width, [(i * members, first + i) for i in range(count)]))
        start += width
    return half, chunks, start


def smoother(members, channels, columns, d_ref, ens_ref, idx_ref, wgt_ref, out_ref, *scratch):
    half, chunks, _ = plan_of(members, columns)
    held, sent, halo, table, total = scratch[:5]
    diag = scratch[5 : 5 + len(chunks)]
    send_sem, recv_sem, halo_send, halo_recv = scratch[5 + len(chunks) :]
    count, tiles = lax.axis_size("cyc"), lax.axis_size("tile")
    mine, tile = lax.axis_index("cyc"), lax.axis_index("tile")
    before, after = lax.rem(mine + count - 1, count), lax.rem(mine + 1, count)
    left, right = lax.rem(tile + tiles - 1, tiles), lax.rem(tile + 1, tiles)
    points = idx_ref.shape[1]

    barrier = pltpu.get_barrier_semaphore()
    for target in ({"cyc": before}, {"cyc": after}, {"tile": left}, {"tile": right}):
        pl.semaphore_signal(barrier, inc=1, device_id=target, device_id_type=MESH)
    pl.semaphore_wait(barrier, 4)

    def onward(number, source):
        start, width, _ = chunks[number]
        return pltpu.make_async_remote_copy(
            src_ref=source.at[:, pl.ds(start, width)],
            dst_ref=held.at[:, pl.ds(start, width)],
            send_sem=send_sem.at[number],
            recv_sem=recv_sem.at[number],
            device_id={"cyc": before},
            device_id_type=MESH,
        )

    def rim(side):
        return pltpu.make_async_remote_copy(
            src_ref=held.at[:, pl.ds(side * half, half)],
            dst_ref=halo.at[:, pl.ds((1 - side) * half, half)],
            send_sem=halo_send.at[side],
            recv_sem=halo_recv.at[side],
            device_id={"tile": (left, right)[side]},
            device_id_type=MESH,
        )

    last = mine == count - 1
    inner = jnp.logical_and(mine > 0, mine < count - 1)

    @pl.when(last)
    def _():
        for number in range(len(chunks)):
            onward(number, d_ref).start()

    @pl.when(inner)
    def _():
        for (start, width, parts), block in zip(chunks, diag):
            lane = lax.broadcasted_iota(jnp.int32, (members, width), 1)
            values = d_ref[:, start : start + width].astype(jnp.float32)
            block[...] = jnp.zeros_like(block)
            for offset, _ in parts:
                inside = jnp.logical_and(lane >= offset, lane < offset + members)
                block[offset : offset + members, :] = jnp.where(inside, values, 0.0).astype(
                    block.dtype
                )

    def apply(source, start, width, parts, first):
        ends = [offset for offset, _ in parts[1:]] + [width]

        def channel(number, carry):
            lanes = pl.ds(pl.multiple_of(number * points, points), points)
            states = ens_ref[:, lanes]
            rows = []
            for (offset, slot), end in zip(parts, ends):
                share = jnp.broadcast_to(table[slot : slot + 1, :], (members, points))
                rows.append(states * share.astype(states.dtype))
                if end > offset + members:
                    rows.append(jnp.zeros((end - offset - members, points), states.dtype))
            product = jnp.dot(
                source[:, start : start + width],
                jnp.concatenate(rows, axis=0),
                preferred_element_type=jnp.float32,
            )
            if first:
                total[:, lanes] = product + states.astype(jnp.float32)
            else:
                total[:, lanes] += product
            return carry

        lax.fori_loop(0, channels, channel, 0)

    @pl.when(jnp.logical_not(last))
    def _():
        weights = wgt_ref[...]
        shares = weights / jnp.sum(weights, axis=0, keepdims=True)
        slots = lax.broadcasted_iota(jnp.int32, table.shape, 0)
        entries = jnp.zeros(table.shape, jnp.float32)
        for corner in range(4):
            entries += jnp.where(
                idx_ref[corner : corner + 1, :] == slots, shares[corner : corner + 1, :], 0.0
            )
        table[...] = entries

    for number, (start, width, parts) in enumerate(chunks):

        @pl.when(jnp.logical_not(last))
        def _(number=number, start=start, width=width):
            onward(number, d_ref).wait_recv()
            if number == 0:
                rim(0).start()
                rim(1).start()

        @pl.when(inner)
        def _(number=number, start=start, width=width):
            lanes = slice(start, start + width)
            later = held[:, lanes]
            product = jnp.dot(later, diag[number][...], preferred_element_type=jnp.float32)
            product += later.astype(jnp.float32) + d_ref[:, lanes].astype(jnp.float32)
            sent[:, lanes] = product.astype(sent.dtype)
            onward(number, sent).start()

        @pl.when(jnp.logical_not(last))
        def _(number=number, start=start, width=width, parts=parts):
            apply(
                held, start, width, [(o, col + RIM_COLS) for o, col in parts], number == 0
            )

    @pl.when(jnp.logical_not(last))
    def _():
        rim(0).wait_recv()
        rim(1).wait_recv()
        parts = [(i * members, i) for i in range(RIM_COLS)]
        parts += [(half + i * members, RIM_COLS + columns + i) for i in range(RIM_COLS)]
        apply(halo, 0, 2 * half, parts, False)
        out_ref[...] = total[...].astype(out_ref.dtype)
        rim(0).wait_send()
        rim(1).wait_send()

    @pl.when(last)
    def _():
        out_ref[...] = ens_ref[...]

    @pl.when(mine > 0)
    def _():
        for number in range(len(chunks)):
            onward(number, d_ref).wait_send()


def on_device(weight_change, ensemble, stencil_index, stencil_weight):
    _, members, _, columns = weight_change.shape
    channels, points = ensemble.shape[2:]
    half, chunks, width = plan_of(members, columns)
    turned = jnp.transpose(weight_change[0], (1, 2, 0))
    pieces = []
    for begin, end in ((0, RIM_COLS), (columns - RIM_COLS, columns)):
        piece = turned[:, begin:end].reshape(members, RIM_COLS * members)
        pieces.append(jnp.pad(piece, ((0, 0), (0, half - piece.shape[1]))))
    for _, wide, parts in chunks[1:]:
        piece = turned[:, parts[0][1] : parts[-1][1] + 1].reshape(members, len(parts) * members)
        pieces.append(jnp.pad(piece, ((0, 0), (0, wide - piece.shape[1]))))
    packed = jnp.concatenate(pieces, axis=1)
    states = ensemble[0].reshape(members, channels * points)
    vmem = pl.BlockSpec(memory_space=pltpu.VMEM)
    result = pl.pallas_call(
        functools.partial(smoother, members, channels, columns),
        out_shape=jax.ShapeDtypeStruct(states.shape, states.dtype),
        in_specs=[vmem] * 4,
        out_specs=vmem,
        scratch_shapes=[
            pltpu.VMEM((members, width), jnp.bfloat16),
            pltpu.VMEM((members, width), jnp.bfloat16),
            pltpu.VMEM((members, 2 * half), jnp.bfloat16),
            pltpu.VMEM((columns + 2 * RIM_COLS, points), jnp.float32),
            pltpu.VMEM(states.shape, jnp.float32),
        ]
        + [pltpu.VMEM((wide, wide), jnp.bfloat16) for _, wide, _ in chunks]
        + [
            pltpu.SemaphoreType.DMA((len(chunks),)),
            pltpu.SemaphoreType.DMA((len(chunks),)),
            pltpu.SemaphoreType.DMA((2,)),
            pltpu.SemaphoreType.DMA((2,)),
        ],
        compiler_params=pltpu.CompilerParams(collective_id=0, has_side_effects=True),
    )(packed, states, stencil_index, stencil_weight)
    return result.reshape(1, members, channels, points)


def solution(mesh):
    placed = (
        P("cyc", None, None, "tile"),
        P("cyc", None, None, "tile"),
        P(None, "tile"),
        P(None, "tile"),
    )
    return jax.shard_map(
        on_device,
        mesh=mesh,
        in_specs=placed,
        out_specs=P("cyc", None, None, "tile"),
        check_vma=False,
    )
```

```python
import functools

import jax
import jax.numpy as jnp
from jax import lax
from jax.experimental import pallas as pl
from jax.experimental.pallas import tpu as pltpu
from jax.sharding import PartitionSpec as P

RIM_COLS = 4
CHUNK = 8
PIECES = 2
MESH = pl.DeviceIdType.MESH


def round_up(value, step):
    return -(-value // step) * step


def plan_of(members, columns):
    half = round_up(RIM_COLS * members, 128)
    edge = [(i * members, i) for i in range(RIM_COLS)]
    edge += [(half + i * members, columns - RIM_COLS + i) for i in range(RIM_COLS)]
    chunks = [(0, 2 * half, edge)]
    start = 2 * half
    for first in range(RIM_COLS, columns - RIM_COLS, CHUNK):
        count = min(CHUNK, columns - RIM_COLS - first)
        width = round_up(count * members, 128)
        chunks.append((start, width, [(i * members, first + i) for i in range(count)]))
        start += width
    return half, chunks, start


def rows_of(members):
    cuts = [min(members, round_up(members * i // PIECES, 16)) for i in range(PIECES + 1)]
    return [(begin, end - begin) for begin, end in zip(cuts, cuts[1:]) if end > begin]


def blocks_of(members, width, parts):
    blocks = []
    for start in range(0, width, 256):
        end = min(width, start + 256)
        offsets = [o for o, _ in parts if o < end and o + members > start]
        low = min(offsets) // 128 * 128
        high = min(width, round_up(max(offsets) + members, 128))
        blocks.append((start, end - start, low, high - low))
    return blocks


def smoother(members, channels, columns, d_ref, ens_ref, idx_ref, wgt_ref, out_ref, *scratch):
    half, chunks, _ = plan_of(members, columns)
    held, sent, halo, table, total = scratch[:5]
    diag = scratch[5 : 5 + len(chunks)]
    send_sem, recv_sem, halo_send, halo_recv = scratch[5 + len(chunks) :]
    count, tiles = lax.axis_size("cyc"), lax.axis_size("tile")
    mine, tile = lax.axis_index("cyc"), lax.axis_index("tile")
    before, after = lax.rem(mine + count - 1, count), lax.rem(mine + 1, count)
    left, right = lax.rem(tile + tiles - 1, tiles), lax.rem(tile + 1, tiles)
    points = idx_ref.shape[1]

    barrier = pltpu.get_barrier_semaphore()
    for target in ({"cyc": before}, {"cyc": after}, {"tile": left}, {"tile": right}):
        pl.semaphore_signal(barrier, inc=1, device_id=target, device_id_type=MESH)
    pl.semaphore_wait(barrier, 4)

    rows = rows_of(members)

    def onward(number, piece, source):
        start, width, _ = chunks[number]
        first, height = rows[piece]
        where = (pl.ds(first, height), pl.ds(start, width))
        return pltpu.make_async_remote_copy(
            src_ref=source.at[where],
            dst_ref=held.at[where],
            send_sem=send_sem.at[number, piece],
            recv_sem=recv_sem.at[number, piece],
            device_id={"cyc": before},
            device_id_type=MESH,
        )

    def rim(side):
        return pltpu.make_async_remote_copy(
            src_ref=held.at[:, pl.ds(side * half, half)],
            dst_ref=halo.at[:, pl.ds((1 - side) * half, half)],
            send_sem=halo_send.at[side],
            recv_sem=halo_recv.at[side],
            device_id={"tile": (left, right)[side]},
            device_id_type=MESH,
        )

    last = mine == count - 1
    inner = jnp.logical_and(mine > 0, mine < count - 1)

    @pl.when(last)
    def _():
        for number in range(len(chunks)):
            for piece in range(len(rows)):
                onward(number, piece, d_ref).start()

    @pl.when(inner)
    def _():
        for (start, width, parts), block in zip(chunks, diag):
            lane = lax.broadcasted_iota(jnp.int32, (members, width), 1)
            values = d_ref[:, start : start + width].astype(jnp.float32)
            block[...] = jnp.zeros_like(block)
            for offset, _ in parts:
                inside = jnp.logical_and(lane >= offset, lane < offset + members)
                block[offset : offset + members, :] = jnp.where(inside, values, 0.0).astype(
                    block.dtype
                )

    def apply(source, start, width, parts, first, begin, end):
        ends = [offset for offset, _ in parts[1:]] + [width]

        def channel(number, carry):
            lanes = pl.ds(pl.multiple_of(number * points, points), points)
            states = ens_ref[:, lanes]
            rows = []
            for (offset, slot), end in zip(parts, ends):
                share = jnp.broadcast_to(table[slot : slot + 1, :], (members, points))
                rows.append(states * share.astype(states.dtype))
                if end > offset + members:
                    rows.append(jnp.zeros((end - offset - members, points), states.dtype))
            product = jnp.dot(
                source[:, start : start + width],
                jnp.concatenate(rows, axis=0),
                preferred_element_type=jnp.float32,
            )
            if first:
                total[:, lanes] = product + states.astype(jnp.float32)
            else:
                total[:, lanes] += product
            return carry

        lax.fori_loop(begin, end, channel, 0, unroll=4)

    @pl.when(jnp.logical_not(last))
    def _():
        weights = wgt_ref[...]
        shares = weights / jnp.sum(weights, axis=0, keepdims=True)
        slots = lax.broadcasted_iota(jnp.int32, table.shape, 0)
        entries = jnp.zeros(table.shape, jnp.float32)
        for corner in range(4):
            entries += jnp.where(
                idx_ref[corner : corner + 1, :] == slots, shares[corner : corner + 1, :], 0.0
            )
        table[...] = entries

    def apply_chunk(number, begin=0, end=channels):
        start, width, parts = chunks[number]
        slots = [(offset, column + RIM_COLS) for offset, column in parts]
        apply(held, start, width, slots, number == 0, begin, end)

    def apply_rim():
        rim(0).wait_recv()
        rim(1).wait_recv()
        parts = [(i * members, i) for i in range(RIM_COLS)]
        parts += [(half + i * members, RIM_COLS + columns + i) for i in range(RIM_COLS)]
        apply(halo, 0, 2 * half, parts, False, 0, channels)

    def finish():
        out_ref[...] = total[...].astype(out_ref.dtype)
        rim(0).wait_send()
        rim(1).wait_send()

    def extend(number, piece):
        start, width, parts = chunks[number]
        first, height = rows[piece]
        across = slice(first, first + height)
        onward(number, piece, sent).wait_recv()
        for lane, size, deep, depth in blocks_of(members, width, parts):
            lanes = slice(start + lane, start + lane + size)
            product = jnp.dot(
                held[across, start + deep : start + deep + depth],
                diag[number][deep : deep + depth, lane : lane + size],
                preferred_element_type=jnp.float32,
            )
            product += held[across, lanes].astype(jnp.float32)
            product += d_ref[across, lanes].astype(jnp.float32)
            sent[across, lanes] = product.astype(sent.dtype)
        onward(number, piece, sent).start()

    @pl.when(inner)
    def _():
        for number in range(len(chunks)):
            for piece in range(len(rows)):
                extend(number, piece)
                if number == 0 and piece == len(rows) - 1:
                    rim(0).start()
                    rim(1).start()
                if number > 0:
                    apply_chunk(
                        number - 1,
                        channels * piece // len(rows),
                        channels * (piece + 1) // len(rows),
                    )
        apply_rim()
        apply_chunk(len(chunks) - 1)
        finish()

    @pl.when(mine == 0)
    def _():
        for number in range(len(chunks)):
            if number == len(chunks) - 1:
                apply_rim()
            for piece in range(len(rows)):
                onward(number, piece, d_ref).wait_recv()
            if number == 0:
                rim(0).start()
                rim(1).start()
            apply_chunk(number)
        finish()

    @pl.when(last)
    def _():
        out_ref[...] = ens_ref[...]

    @pl.when(mine > 0)
    def _():
        for number in range(len(chunks)):
            for piece in range(len(rows)):
                onward(number, piece, d_ref).wait_send()


def on_device(weight_change, ensemble, stencil_index, stencil_weight):
    _, members, _, columns = weight_change.shape
    channels, points = ensemble.shape[2:]
    half, chunks, width = plan_of(members, columns)
    turned = jnp.transpose(weight_change[0], (1, 2, 0))
    pieces = []
    for begin, end in ((0, RIM_COLS), (columns - RIM_COLS, columns)):
        piece = turned[:, begin:end].reshape(members, RIM_COLS * members)
        pieces.append(jnp.pad(piece, ((0, 0), (0, half - piece.shape[1]))))
    for _, wide, parts in chunks[1:]:
        piece = turned[:, parts[0][1] : parts[-1][1] + 1].reshape(members, len(parts) * members)
        pieces.append(jnp.pad(piece, ((0, 0), (0, wide - piece.shape[1]))))
    packed = jnp.concatenate(pieces, axis=1)
    states = ensemble[0].reshape(members, channels * points)
    vmem = pl.BlockSpec(memory_space=pltpu.VMEM)
    result = pl.pallas_call(
        functools.partial(smoother, members, channels, columns),
        out_shape=jax.ShapeDtypeStruct(states.shape, states.dtype),
        in_specs=[vmem] * 4,
        out_specs=vmem,
        scratch_shapes=[
            pltpu.VMEM((members, width), jnp.bfloat16),
            pltpu.VMEM((members, width), jnp.bfloat16),
            pltpu.VMEM((members, 2 * half), jnp.bfloat16),
            pltpu.VMEM((columns + 2 * RIM_COLS, points), jnp.float32),
            pltpu.VMEM(states.shape, jnp.float32),
        ]
        + [pltpu.VMEM((wide, wide), jnp.bfloat16) for _, wide, _ in chunks]
        + [
            pltpu.SemaphoreType.DMA((len(chunks), PIECES)),
            pltpu.SemaphoreType.DMA((len(chunks), PIECES)),
            pltpu.SemaphoreType.DMA((2,)),
            pltpu.SemaphoreType.DMA((2,)),
        ],
        compiler_params=pltpu.CompilerParams(collective_id=0, has_side_effects=True),
    )(packed, states, stencil_index, stencil_weight)
    return result.reshape(1, members, channels, points)


def solution(mesh):
    placed = (
        P("cyc", None, None, "tile"),
        P("cyc", None, None, "tile"),
        P(None, "tile"),
        P(None, "tile"),
    )
    return jax.shard_map(
        on_device,
        mesh=mesh,
        in_specs=placed,
        out_specs=P("cyc", None, None, "tile"),
        check_vma=False,
    )
```

```python
import functools

import jax
import jax.numpy as jnp
from jax import lax
from jax.experimental import pallas as pl
from jax.experimental.pallas import tpu as pltpu
from jax.sharding import PartitionSpec as P

RIM_COLS = 4
CHUNK = 8
PIECES = 2
MESH = pl.DeviceIdType.MESH


def round_up(value, step):
    return -(-value // step) * step


def plan_of(members, columns):
    half = round_up(RIM_COLS * members, 128)
    edge = [(i * members, i) for i in range(RIM_COLS)]
    edge += [(half + i * members, columns - RIM_COLS + i) for i in range(RIM_COLS)]
    chunks = [(0, 2 * half, edge)]
    start = 2 * half
    for first in range(RIM_COLS, columns - RIM_COLS, CHUNK):
        count = min(CHUNK, columns - RIM_COLS - first)
        width = round_up(count * members, 128)
        chunks.append((start, width, [(i * members, first + i) for i in range(count)]))
        start += width
    return half, chunks, start


def rows_of(members):
    cuts = [min(members, round_up(members * i // PIECES, 16)) for i in range(PIECES + 1)]
    return [(begin, end - begin) for begin, end in zip(cuts, cuts[1:]) if end > begin]


def blocks_of(members, width, parts):
    blocks = []
    for start in range(0, width, 256):
        end = min(width, start + 256)
        offsets = [o for o, _ in parts if o < end and o + members > start]
        low = min(offsets) // 128 * 128
        high = min(width, round_up(max(offsets) + members, 128))
        blocks.append((start, end - start, low, high - low))
    return blocks


def smoother(members, channels, columns, d_any, ens_any, idx_ref, wgt_ref, out_ref, *scratch):
    half, chunks, _ = plan_of(members, columns)
    held, sent, halo, table, total, flat, d_ref, ens_ref = scratch[:8]
    diag = scratch[8 : 8 + len(chunks)]
    send_sem, recv_sem, halo_send, halo_recv, load_sem = scratch[8 + len(chunks) :]
    count, tiles = lax.axis_size("cyc"), lax.axis_size("tile")
    mine, tile = lax.axis_index("cyc"), lax.axis_index("tile")
    before, after = lax.rem(mine + count - 1, count), lax.rem(mine + 1, count)
    left, right = lax.rem(tile + tiles - 1, tiles), lax.rem(tile + 1, tiles)
    points = idx_ref.shape[1]

    barrier = pltpu.get_barrier_semaphore()
    for target in ({"cyc": before}, {"cyc": after}, {"tile": left}, {"tile": right}):
        pl.semaphore_signal(barrier, inc=1, device_id=target, device_id_type=MESH)
    last = mine == count - 1
    inner = jnp.logical_and(mine > 0, mine < count - 1)
    load_d = pltpu.make_async_copy(d_any, d_ref, load_sem.at[0])
    load_states = pltpu.make_async_copy(ens_any, ens_ref, load_sem.at[1])

    @pl.when(inner)
    def _():
        load_d.start()

    @pl.when(jnp.logical_not(last))
    def _():
        load_states.start()

    pl.semaphore_wait(barrier, 4)

    rows = rows_of(members)

    def onward(number, piece, source):
        start, width, _ = chunks[number]
        first, height = rows[piece]
        where = (pl.ds(first, height), pl.ds(start, width))
        return pltpu.make_async_remote_copy(
            src_ref=source.at[where],
            dst_ref=held.at[where],
            send_sem=send_sem.at[number, piece],
            recv_sem=recv_sem.at[number, piece],
            device_id={"cyc": before},
            device_id_type=MESH,
        )

    def rim(side):
        return pltpu.make_async_remote_copy(
            src_ref=held.at[:, pl.ds(side * half, half)],
            dst_ref=halo.at[:, pl.ds((1 - side) * half, half)],
            send_sem=halo_send.at[side],
            recv_sem=halo_recv.at[side],
            device_id={"tile": (left, right)[side]},
            device_id_type=MESH,
        )

    @pl.when(last)
    def _():
        for number in range(len(chunks)):
            for piece in range(len(rows)):
                onward(number, piece, d_any).start()

    @pl.when(inner)
    def _():
        load_d.wait()
        for (start, width, parts), block in zip(chunks, diag):
            lane = lax.broadcasted_iota(jnp.int32, (members, width), 1)
            values = d_ref[:, start : start + width].astype(jnp.float32)
            block[...] = jnp.zeros_like(block)
            for offset, _ in parts:
                inside = jnp.logical_and(lane >= offset, lane < offset + members)
                block[offset : offset + members, :] = jnp.where(inside, values, 0.0).astype(
                    block.dtype
                )

    def apply(source, start, width, parts, begin, end):
        ends = [offset for offset, _ in parts[1:]] + [width]

        def channel(number, carry):
            lanes = pl.ds(pl.multiple_of(number * points, points), points)
            states = flat[:, lanes]
            rows = []
            for (offset, slot), end in zip(parts, ends):
                share = jnp.broadcast_to(table[slot : slot + 1, :], (members, points))
                rows.append(states * share.astype(states.dtype))
                if end > offset + members:
                    rows.append(jnp.zeros((end - offset - members, points), states.dtype))
            product = jnp.dot(
                source[:, start : start + width],
                jnp.concatenate(rows, axis=0),
                preferred_element_type=jnp.float32,
            )
            for block in range(points // 128):
                total[block, pl.ds(number, members, stride=channels), :] += product[
                    :, block * 128 : (block + 1) * 128
                ]
            return carry

        lax.fori_loop(begin, end, channel, 0, unroll=4)

    @pl.when(jnp.logical_not(last))
    def _():
        weights = wgt_ref[...]
        shares = weights / jnp.sum(weights, axis=0, keepdims=True)
        slots = lax.broadcasted_iota(jnp.int32, table.shape, 0)
        entries = jnp.zeros(table.shape, jnp.float32)
        for corner in range(4):
            entries += jnp.where(
                idx_ref[corner : corner + 1, :] == slots, shares[corner : corner + 1, :], 0.0
            )
        table[...] = entries
        load_states.wait()
        for block in range(points // 128):
            states = ens_ref[:, :, block * 128 : (block + 1) * 128].astype(jnp.float32)
            total[block] = states.reshape(members * channels, 128)
            for number in range(channels):
                states = total[block, pl.ds(number, members, stride=channels), :]
                begin = number * points + block * 128
                flat[:, begin : begin + 128] = states.astype(flat.dtype)
        total[...] = jnp.zeros_like(total)

    def apply_chunk(number, begin=0, end=channels):
        start, width, parts = chunks[number]
        slots = [(offset, column + RIM_COLS) for offset, column in parts]
        apply(held, start, width, slots, begin, end)

    def apply_rim():
        rim(0).wait_recv()
        rim(1).wait_recv()
        parts = [(i * members, i) for i in range(RIM_COLS)]
        parts += [(half + i * members, RIM_COLS + columns + i) for i in range(RIM_COLS)]
        apply(halo, 0, 2 * half, parts, 0, channels)

    def finish():
        for block in range(points // 128):
            out_ref[:, :, block * 128 : (block + 1) * 128] = (
                total[block].reshape(members, channels, 128).astype(out_ref.dtype)
            )
        rim(0).wait_send()
        rim(1).wait_send()

    def extend(number, piece):
        start, width, parts = chunks[number]
        first, height = rows[piece]
        across = slice(first, first + height)
        onward(number, piece, sent).wait_recv()
        for lane, size, deep, depth in blocks_of(members, width, parts):
            lanes = slice(start + lane, start + lane + size)
            product = jnp.dot(
                held[across, start + deep : start + deep + depth],
                diag[number][deep : deep + depth, lane : lane + size],
                preferred_element_type=jnp.float32,
            )
            product += held[across, lanes].astype(jnp.float32)
            product += d_ref[across, lanes].astype(jnp.float32)
            sent[across, lanes] = product.astype(sent.dtype)
        onward(number, piece, sent).start()

    @pl.when(inner)
    def _():
        for number in range(len(chunks)):
            for piece in range(len(rows)):
                extend(number, piece)
                if number == 0 and piece == len(rows) - 1:
                    rim(0).start()
                    rim(1).start()
                if number > 0:
                    apply_chunk(
                        number - 1,
                        channels * piece // len(rows),
                        channels * (piece + 1) // len(rows),
                    )
        apply_rim()
        apply_chunk(len(chunks) - 1)
        finish()

    @pl.when(mine == 0)
    def _():
        for number in range(len(chunks)):
            if number == len(chunks) - 1:
                apply_rim()
            for piece in range(len(rows)):
                onward(number, piece, sent).wait_recv()
            if number == 0:
                rim(0).start()
                rim(1).start()
            apply_chunk(number)
        finish()

    @pl.when(last)
    def _():
        out_ref[...] = jnp.zeros_like(out_ref)

    @pl.when(mine > 0)
    def _():
        for number in range(len(chunks)):
            for piece in range(len(rows)):
                onward(number, piece, sent).wait_send()


def on_device(weight_change, ensemble, stencil_index, stencil_weight):
    _, members, _, columns = weight_change.shape
    channels, points = ensemble.shape[2:]
    half, chunks, width = plan_of(members, columns)
    turned = jnp.transpose(weight_change[0], (1, 2, 0))
    pieces = []
    for begin, end in ((0, RIM_COLS), (columns - RIM_COLS, columns)):
        piece = turned[:, begin:end].reshape(members, RIM_COLS * members)
        pieces.append(jnp.pad(piece, ((0, 0), (0, half - piece.shape[1]))))
    for _, wide, parts in chunks[1:]:
        piece = turned[:, parts[0][1] : parts[-1][1] + 1].reshape(members, len(parts) * members)
        pieces.append(jnp.pad(piece, ((0, 0), (0, wide - piece.shape[1]))))
    packed = jnp.concatenate(pieces, axis=1)
    states = ensemble[0]
    vmem = pl.BlockSpec(memory_space=pltpu.VMEM)
    anywhere = pl.BlockSpec(memory_space=pl.ANY)
    result = pl.pallas_call(
        functools.partial(smoother, members, channels, columns),
        out_shape=pltpu.VMEM(states.shape, states.dtype),
        in_specs=[vmem, anywhere] + [vmem] * 2,
        out_specs=vmem,
        scratch_shapes=[
            pltpu.VMEM((members, width), jnp.bfloat16),
            pltpu.VMEM((members, width), jnp.bfloat16),
            pltpu.VMEM((members, 2 * half), jnp.bfloat16),
            pltpu.VMEM((columns + 2 * RIM_COLS, points), jnp.float32),
            pltpu.VMEM((points // 128, members * channels, 128), jnp.float32),
            pltpu.VMEM((members, channels * points), jnp.bfloat16),
            pltpu.VMEM((members, width), jnp.bfloat16),
            pltpu.VMEM(states.shape, jnp.bfloat16),
        ]
        + [pltpu.VMEM((wide, wide), jnp.bfloat16) for _, wide, _ in chunks]
        + [
            pltpu.SemaphoreType.DMA((len(chunks), PIECES)),
            pltpu.SemaphoreType.DMA((len(chunks), PIECES)),
            pltpu.SemaphoreType.DMA((2,)),
            pltpu.SemaphoreType.DMA((2,)),
            pltpu.SemaphoreType.DMA((2,)),
        ],
        compiler_params=pltpu.CompilerParams(collective_id=0, has_side_effects=True),
    )(
        pltpu.with_memory_space_constraint(packed, pltpu.VMEM),
        states,
        stencil_index,
        stencil_weight,
    )
    total = states.astype(jnp.float32) + result.astype(jnp.float32)
    return total.astype(states.dtype)[None]


def solution(mesh):
    placed = (
        P("cyc", None, None, "tile"),
        P("cyc", None, None, "tile"),
        P(None, "tile"),
        P(None, "tile"),
    )
    return jax.shard_map(
        on_device,
        mesh=mesh,
        in_specs=placed,
        out_specs=P("cyc", None, None, "tile"),
        check_vma=False,
    )
```

```python
import functools

import jax
import jax.numpy as jnp
from jax import lax
from jax.experimental import pallas as pl
from jax.experimental.pallas import tpu as pltpu
from jax.sharding import PartitionSpec as P

RIM_COLS = 4
CHUNK = 8
PIECES = 3
MESH = pl.DeviceIdType.MESH


def round_up(value, step):
    return -(-value // step) * step


def plan_of(members, columns):
    half = round_up(RIM_COLS * members, 128)
    edge = [(i * members, i) for i in range(RIM_COLS)]
    edge += [(half + i * members, columns - RIM_COLS + i) for i in range(RIM_COLS)]
    chunks = [(0, 2 * half, edge)]
    start = 2 * half
    for first in range(RIM_COLS, columns - RIM_COLS, CHUNK):
        count = min(CHUNK, columns - RIM_COLS - first)
        width = round_up(count * members, 128)
        chunks.append((start, width, [(i * members, first + i) for i in range(count)]))
        start += width
    return half, chunks, start


def rows_of(members):
    cuts = [min(members, round_up(members * i // PIECES, 16)) for i in range(PIECES + 1)]
    return [(begin, end - begin) for begin, end in zip(cuts, cuts[1:]) if end > begin]


def blocks_of(members, width, parts):
    blocks = []
    for start in range(0, width, 256):
        end = min(width, start + 256)
        offsets = [o for o, _ in parts if o < end and o + members > start]
        low = min(offsets) // 128 * 128
        high = min(width, round_up(max(offsets) + members, 128))
        blocks.append((start, end - start, low, high - low))
    return blocks


def smoother(members, channels, columns, d_any, ens_any, idx_ref, wgt_ref, out_ref, *scratch):
    half, chunks, _ = plan_of(members, columns)
    held, sent, halo, table, total, flat, d_ref, ens_ref = scratch[:8]
    diag = scratch[8 : 8 + len(chunks)]
    send_sem, recv_sem, halo_send, halo_recv, load_sem = scratch[8 + len(chunks) :]
    count, tiles = lax.axis_size("cyc"), lax.axis_size("tile")
    mine, tile = lax.axis_index("cyc"), lax.axis_index("tile")
    before, after = lax.rem(mine + count - 1, count), lax.rem(mine + 1, count)
    left, right = lax.rem(tile + tiles - 1, tiles), lax.rem(tile + 1, tiles)
    points = idx_ref.shape[1]

    barrier = pltpu.get_barrier_semaphore()
    for target in ({"cyc": before}, {"cyc": after}, {"tile": left}, {"tile": right}):
        pl.semaphore_signal(barrier, inc=1, device_id=target, device_id_type=MESH)
    last = mine == count - 1
    inner = jnp.logical_and(mine > 0, mine < count - 1)
    load_d = pltpu.make_async_copy(d_any, d_ref, load_sem.at[0])
    load_states = pltpu.make_async_copy(ens_any, ens_ref, load_sem.at[1])

    @pl.when(inner)
    def _():
        load_d.start()

    @pl.when(jnp.logical_not(last))
    def _():
        load_states.start()

    pl.semaphore_wait(barrier, 4)

    rows = rows_of(members)

    def onward(number, piece, source):
        start, width, _ = chunks[number]
        first, height = rows[piece]
        where = (pl.ds(first, height), pl.ds(start, width))
        return pltpu.make_async_remote_copy(
            src_ref=source.at[where],
            dst_ref=held.at[where],
            send_sem=send_sem.at[number, piece],
            recv_sem=recv_sem.at[number, piece],
            device_id={"cyc": before},
            device_id_type=MESH,
        )

    def rim(side):
        return pltpu.make_async_remote_copy(
            src_ref=held.at[:, pl.ds(side * half, half)],
            dst_ref=halo.at[:, pl.ds((1 - side) * half, half)],
            send_sem=halo_send.at[side],
            recv_sem=halo_recv.at[side],
            device_id={"tile": (left, right)[side]},
            device_id_type=MESH,
        )

    @pl.when(last)
    def _():
        for number in range(len(chunks)):
            for piece in range(len(rows)):
                onward(number, piece, d_any).start()

    @pl.when(inner)
    def _():
        load_d.wait()
        for (start, width, parts), block in zip(chunks, diag):
            lane = lax.broadcasted_iota(jnp.int32, (members, width), 1)
            values = d_ref[:, start : start + width].astype(jnp.float32)
            block[...] = jnp.zeros_like(block)
            for offset, _ in parts:
                inside = jnp.logical_and(lane >= offset, lane < offset + members)
                block[offset : offset + members, :] = jnp.where(inside, values, 0.0).astype(
                    block.dtype
                )

    def apply(source, start, width, parts, begin, end):
        ends = [offset for offset, _ in parts[1:]] + [width]

        def channel(number, carry):
            lanes = pl.ds(pl.multiple_of(number * points, points), points)
            states = flat[:, lanes]
            rows = []
            for (offset, slot), end in zip(parts, ends):
                share = jnp.broadcast_to(table[slot : slot + 1, :], (members, points))
                rows.append(states * share.astype(states.dtype))
                if end > offset + members:
                    rows.append(jnp.zeros((end - offset - members, points), states.dtype))
            product = jnp.dot(
                source[:, start : start + width],
                jnp.concatenate(rows, axis=0),
                preferred_element_type=jnp.float32,
            )
            for block in range(points // 128):
                total[block, pl.ds(number, members, stride=channels), :] += product[
                    :, block * 128 : (block + 1) * 128
                ]
            return carry

        lax.fori_loop(begin, end, channel, 0, unroll=4)

    @pl.when(jnp.logical_not(last))
    def _():
        weights = wgt_ref[...]
        shares = weights / jnp.sum(weights, axis=0, keepdims=True)
        slots = lax.broadcasted_iota(jnp.int32, table.shape, 0)
        entries = jnp.zeros(table.shape, jnp.float32)
        for corner in range(4):
            entries += jnp.where(
                idx_ref[corner : corner + 1, :] == slots, shares[corner : corner + 1, :], 0.0
            )
        table[...] = entries
        load_states.wait()
        for block in range(points // 128):
            states = ens_ref[:, :, block * 128 : (block + 1) * 128].astype(jnp.float32)
            total[block] = states.reshape(members * channels, 128)
            for number in range(channels):
                states = total[block, pl.ds(number, members, stride=channels), :]
                begin = number * points + block * 128
                flat[:, begin : begin + 128] = states.astype(flat.dtype)
        total[...] = jnp.zeros_like(total)

    def apply_chunk(number, begin=0, end=channels):
        start, width, parts = chunks[number]
        slots = [(offset, column + RIM_COLS) for offset, column in parts]
        apply(held, start, width, slots, begin, end)

    def apply_rim():
        rim(0).wait_recv()
        rim(1).wait_recv()
        parts = [(i * members, i) for i in range(RIM_COLS)]
        parts += [(half + i * members, RIM_COLS + columns + i) for i in range(RIM_COLS)]
        apply(halo, 0, 2 * half, parts, 0, channels)

    def finish():
        for block in range(points // 128):
            out_ref[:, :, block * 128 : (block + 1) * 128] = (
                total[block].reshape(members, channels, 128).astype(out_ref.dtype)
            )
        rim(0).wait_send()
        rim(1).wait_send()

    def extend(number, piece):
        start, width, parts = chunks[number]
        first, height = rows[piece]
        across = slice(first, first + height)
        onward(number, piece, sent).wait_recv()
        for lane, size, deep, depth in blocks_of(members, width, parts):
            lanes = slice(start + lane, start + lane + size)
            product = jnp.dot(
                held[across, start + deep : start + deep + depth],
                diag[number][deep : deep + depth, lane : lane + size],
                preferred_element_type=jnp.float32,
            )
            product += held[across, lanes].astype(jnp.float32)
            product += d_ref[across, lanes].astype(jnp.float32)
            sent[across, lanes] = product.astype(sent.dtype)
        onward(number, piece, sent).start()

    @pl.when(inner)
    def _():
        middle = channels // 2
        tasks = [
            (number, begin, end)
            for number in range(len(chunks))
            for begin, end in ((0, middle), (middle, channels))
        ]
        for number in range(len(chunks)):
            for piece in range(len(rows)):
                extend(number, piece)
                if number == 0 and piece == len(rows) - 1:
                    rim(0).start()
                    rim(1).start()
                if piece in (1,) and tasks and tasks[0][0] < number - 0:
                    apply_chunk(*tasks.pop(0))
        apply_rim()
        for task in tasks:
            apply_chunk(*task)
        finish()

    @pl.when(mine == 0)
    def _():
        for number in range(len(chunks)):
            if number == len(chunks) - 1:
                apply_rim()
            for piece in range(len(rows)):
                onward(number, piece, sent).wait_recv()
            if number == 0:
                rim(0).start()
                rim(1).start()
            apply_chunk(number)
        finish()

    @pl.when(last)
    def _():
        out_ref[...] = jnp.zeros_like(out_ref)

    @pl.when(mine > 0)
    def _():
        for number in range(len(chunks)):
            for piece in range(len(rows)):
                onward(number, piece, sent).wait_send()


def on_device(weight_change, ensemble, stencil_index, stencil_weight):
    _, members, _, columns = weight_change.shape
    channels, points = ensemble.shape[2:]
    half, chunks, width = plan_of(members, columns)
    turned = jnp.transpose(weight_change[0], (1, 2, 0))
    pieces = []
    for begin, end in ((0, RIM_COLS), (columns - RIM_COLS, columns)):
        piece = turned[:, begin:end].reshape(members, RIM_COLS * members)
        pieces.append(jnp.pad(piece, ((0, 0), (0, half - piece.shape[1]))))
    for _, wide, parts in chunks[1:]:
        piece = turned[:, parts[0][1] : parts[-1][1] + 1].reshape(members, len(parts) * members)
        pieces.append(jnp.pad(piece, ((0, 0), (0, wide - piece.shape[1]))))
    packed = jnp.concatenate(pieces, axis=1)
    states = ensemble[0]
    vmem = pl.BlockSpec(memory_space=pltpu.VMEM)
    anywhere = pl.BlockSpec(memory_space=pl.ANY)
    result = pl.pallas_call(
        functools.partial(smoother, members, channels, columns),
        out_shape=pltpu.VMEM(states.shape, states.dtype),
        in_specs=[vmem, anywhere] + [vmem] * 2,
        out_specs=vmem,
        scratch_shapes=[
            pltpu.VMEM((members, width), jnp.bfloat16),
            pltpu.VMEM((members, width), jnp.bfloat16),
            pltpu.VMEM((members, 2 * half), jnp.bfloat16),
            pltpu.VMEM((columns + 2 * RIM_COLS, points), jnp.float32),
            pltpu.VMEM((points // 128, members * channels, 128), jnp.float32),
            pltpu.VMEM((members, channels * points), jnp.bfloat16),
            pltpu.VMEM((members, width), jnp.bfloat16),
            pltpu.VMEM(states.shape, jnp.bfloat16),
        ]
        + [pltpu.VMEM((wide, wide), jnp.bfloat16) for _, wide, _ in chunks]
        + [
            pltpu.SemaphoreType.DMA((len(chunks), PIECES)),
            pltpu.SemaphoreType.DMA((len(chunks), PIECES)),
            pltpu.SemaphoreType.DMA((2,)),
            pltpu.SemaphoreType.DMA((2,)),
            pltpu.SemaphoreType.DMA((2,)),
        ],
        compiler_params=pltpu.CompilerParams(collective_id=0, has_side_effects=True),
    )(
        pltpu.with_memory_space_constraint(packed, pltpu.VMEM),
        states,
        stencil_index,
        stencil_weight,
    )
    total = states.astype(jnp.float32) + result.astype(jnp.float32)
    return total.astype(states.dtype)[None]


def solution(mesh):
    placed = (
        P("cyc", None, None, "tile"),
        P("cyc", None, None, "tile"),
        P(None, "tile"),
        P(None, "tile"),
    )
    return jax.shard_map(
        on_device,
        mesh=mesh,
        in_specs=placed,
        out_specs=P("cyc", None, None, "tile"),
        check_vma=False,
    )
```
